32 devices in a mesh: section: 4 (over y, x), state: 8 (over z, core).
Axes of the slice: x: 2, y: 2, z: 4, core: 2. Of those that a mesh axis runs over, the one named last changes fastest.
Arguments:
- belief: float32 [4, 512, 2048], P('section', None, 'state'), may hold values from 0 to 0.04
- action: int32 [4, 512], P('section'), may hold values from 0 to 7
- next_index: int32 [4, 512, 32], P('section'), may hold values from 0 to 511, as said below
- obs_table: float32 [8, 32, 2048], P(None, None, 'state'), may hold values from -1 to 1
- transition: bfloat16 [8, 2048, 2048], P(None, 'state'), may hold values from -0.1875 to 0.1875
- reward: float32 [8, 2048], P(None, 'state'), may hold values from -6 to 6
- terminal: float32 [512, 2048], P(None, 'state'), may hold values from -6 to 6
Outputs:
- alphas: float32 [4, 512, 2048], P('section', None, 'state')
- values: float32 [4, 512], P('section')
The draws below stay inside these ranges and needn't reach their ends.
Inputs may be any that keep to these rules, and one draw needn't show every extreme that they name: next_index[h, b, o] < 128 * (b // 128 + 1): a belief of micro-batch m names only next-section alpha vectors of micro-batches 0 to m.
All inputs are finite; a program needn't handle non-finite values.
Results may differ from the reference program's by a relative error of at most 0.012.
Values sent between devices are 32-bit elements; how exact they have to be, the bound alone decides.
No kernel may reach another device: no remote copies, remote signals or barrier semaphores. Data moves between devices by JAX's collectives and lax.ppermute only.
A program may use at most 64 MiB of HBM per device.

```python
import jax
import jax.numpy as jnp
from jax import lax

S = 2048
A = 8
OBS = 32
K = 512
BLOCK = 128
HORIZON = 4


def draw_next_index(key, part):
    rows = jnp.arange(K, dtype=jnp.int32)
    upper = (rows // BLOCK + 1) * BLOCK
    upper = jnp.broadcast_to(upper[None, :, None], (HORIZON, K, OBS))
    return jax.random.randint(jax.random.fold_in(key, 11), (HORIZON, K, OBS), 0, upper, dtype=jnp.int32)


def with_ends(result, key, low, largest):
    spot = [jax.random.randint(jax.random.fold_in(key, axis), (), 0, length) for axis, length in enumerate(result.shape)]
    main_axis = result.shape.index(max(result.shape))
    beside = spot[:main_axis] + [(spot[main_axis] + 1) % result.shape[main_axis]] + spot[main_axis + 1:]
    return result.at[tuple(spot)].set(low).at[tuple(beside)].set(largest)


def raised(entries, stream_key, source, target, shards_of, factor):
    def block_of(dim):
        return (jnp.arange(entries.shape[dim]) // (entries.shape[dim] // shards_of)).reshape((-1,) + (1,) * (entries.ndim - 1 - dim))

    first = jax.random.permutation(stream_key, shards_of)[block_of(target)]
    second = (block_of(target) + shards_of // 2) % shards_of
    return jnp.where((block_of(source) == first) | (block_of(source) == second), factor * entries, entries)


def level_of(key, extent, cuts, least, high):
    loudness = 1.0
    for position, shards_of in cuts:
        draws = jax.random.uniform(jax.random.fold_in(jax.random.fold_in(key, 6), position), (shards_of,), jnp.float32, least / len(cuts), high / len(cuts))
        loudness = loudness * jnp.repeat(jnp.exp(draws), extent[position] // shards_of).reshape((-1,) + (1,) * (len(extent) - 1 - position))
    return loudness


def gaussian(own_key, dims, deviation, reach, cuts=(), held_as=jnp.bfloat16):
    drawn = jax.random.normal(own_key, dims, jnp.float32) * deviation
    if len(cuts) > 0:
        drawn = level_of(own_key, dims, cuts, -0.22, 0.18) * drawn
    return jnp.clip(drawn, min=-reach, max=reach).astype(held_as)


def gaussian_with(rng, extent, width, most, split, heavy, kind=jnp.bfloat16):
    drawn = width * jax.random.normal(rng, extent, jnp.float32)
    if split:
        drawn = drawn * level_of(rng, extent, split, -0.22, 0.18)
    return jnp.clip(raised(drawn, jax.random.fold_in(rng, 3), *heavy), -most, most).astype(kind)


def setup_inputs(seed: int = 0) -> dict:
    key_of = jax.random.split(jax.random.key(seed), 8)
    return {
        "belief": jnp.clip(0.04 * jax.random.uniform(key_of[0], (HORIZON, K, S), jnp.float32) ** level_of(key_of[0], (HORIZON, K, S), ((0, 4), (2, 8)), -0.2, 0.2), 0.0, 0.04),
        "action": with_ends(jax.random.randint(key_of[1], (HORIZON, K), 0, A), jax.random.fold_in(key_of[1], 1), 0, A - 1).astype(jnp.int32),
        "next_index": draw_next_index(jax.random.fold_in(key_of[7], 71), 0),
        "obs_table": gaussian(key_of[3], (A, OBS, S), OBS ** -0.5, 1.0, ((2, 8),), jnp.float32),
        "transition": gaussian_with(key_of[4], (A, S, S), S ** -0.5, 0.1875, ((1, 8),), (1, 2, 8, 2.0)),
        "reward": gaussian(key_of[5], (A, S), 1.0, 6.0, ((1, 8),), jnp.float32),
        "terminal": gaussian(key_of[6], (K, S), 1.0, 6.0, ((1, 8),), jnp.float32),
    }


discount = 0.95


def backup(next_alphas, act_rows, next_rows, obs_table, trans_flat, reward):
    picked = next_alphas[next_rows]
    per_action = jnp.einsum('bos,aos->bas', picked, obs_table, precision=lax.Precision.HIGHEST)
    onehot = (act_rows[:, None] == jnp.arange(A, dtype=jnp.int32)[None, :]).astype(jnp.float32)
    masked = (per_action * onehot[:, :, None]).astype(jnp.bfloat16).reshape(act_rows.shape[0], A * S)
    summed = jnp.dot(masked, trans_flat, preferred_element_type=jnp.float32)
    reward_rows = jnp.dot(onehot, reward, precision=lax.Precision.HIGHEST)
    return reward_rows + discount * summed


def reference(belief, action, next_index, obs_table, transition, reward, terminal):
    trans_flat = transition.reshape(A * S, S)
    nextset = terminal
    alpha_list = [None] * HORIZON
    value_list = [None] * HORIZON
    for section_number in reversed(range(HORIZON)):
        act_blocks = action[section_number].reshape(K // BLOCK, BLOCK)
        next_blocks = next_index[section_number].reshape(K // BLOCK, BLOCK, OBS)

        def one_block(pieces, nextset=nextset):
            return backup(nextset, pieces[0], pieces[1], obs_table, trans_flat, reward)

        section_alphas = lax.map(one_block, (act_blocks, next_blocks)).reshape(K, S)
        alpha_list[section_number] = section_alphas
        value_list[section_number] = jnp.sum(belief[section_number] * section_alphas, axis=1)
        nextset = section_alphas
    return jnp.stack(alpha_list), jnp.stack(value_list)
```

```python
import functools

import jax
import jax.numpy as jnp
from jax import lax
from jax.experimental import pallas as pl
from jax.experimental.pallas import tpu as pltpu
from jax.sharding import PartitionSpec as P

discount = 0.95


VMEM = pl.BlockSpec(memory_space=pltpu.VMEM)
ANY = pl.BlockSpec(memory_space=pl.ANY)


def swap(x, axis, distance):
    size = lax.axis_size(axis)
    return lax.ppermute(x, axis, [(i, i ^ distance) for i in range(size)])


def place():
    group = lax.axis_index("section")
    state = lax.axis_index("state")
    return group, state // 2, state % 2


def columns_of(t_ref, block, width):
    start = pl.multiple_of(block * width, width)
    return t_ref[:, pl.ds(start, width)]


def pick_kernel(section, groups, observations, actions, whole_next, *refs):
    index_refs, refs = refs[:groups], refs[groups:]
    next_count = 1 if whole_next else groups
    next_refs, refs = refs[:next_count], refs[next_count:]
    obs_ref, t_ref, masked_ref, send_ref, index_scratch, next_scratch = refs
    group, chip, core = place()
    share, width = masked_ref.shape[0], obs_ref.shape[2]
    for d in range(groups):

        @pl.when((group ^ section) == d)
        def _(d=d):
            index_scratch[0 : observations + 8, 0:share] = index_refs[d][...]

    if whole_next:
        next_scratch[...] = next_refs[0][...].astype(jnp.bfloat16)
    else:
        for d in range(groups):
            start = pl.multiple_of((group ^ d) * share, share)
            next_scratch[pl.ds(start, share), :] = next_refs[d][...].astype(jnp.bfloat16)
    rows = jnp.transpose(index_scratch[...])[0:share]
    chosen = rows[:, observations : observations + 1]
    names = lax.broadcasted_iota(jnp.int32, (share, next_scratch.shape[0]), 1)
    kinds = lax.broadcasted_iota(jnp.int32, (share, 2 * actions), 1)
    action_hot = ((kinds == chosen) | (kinds == chosen + actions)).astype(jnp.bfloat16)
    next_rows = next_scratch[...]
    total = jnp.zeros((share, width), jnp.float32)
    for o in range(observations):
        hot = (names == rows[:, o : o + 1]).astype(jnp.float32).astype(jnp.bfloat16)
        picked = jnp.dot(hot, next_rows, preferred_element_type=jnp.float32)
        table = obs_ref[:, o, :]
        high = table.astype(jnp.bfloat16)
        low = (table - high.astype(jnp.float32)).astype(jnp.bfloat16)
        weights = jnp.dot(
            action_hot, jnp.concatenate([high, low], axis=0), preferred_element_type=jnp.float32
        )
        total = total + picked * weights
    for a in range(actions):
        masked_ref[:, a * width : (a + 1) * width] = jnp.where(chosen == a, total, 0.0).astype(
            jnp.bfloat16
        )
    masked = masked_ref[...]
    for d in range(send_ref.shape[0]):
        send_ref[d] = jnp.dot(
            masked,
            columns_of(t_ref, (chip ^ d) * 2 + (1 - core), width),
            preferred_element_type=jnp.float32,
        )


def keep_kernel(masked_ref, t_ref, keep_ref):
    _, chip, core = place()
    masked = masked_ref[...]
    for d in range(keep_ref.shape[0]):
        keep_ref[d] = jnp.dot(
            masked,
            columns_of(t_ref, (chip ^ d) * 2 + core, keep_ref.shape[2]),
            preferred_element_type=jnp.float32,
        )


def last_kernel(groups, *refs):
    pieces, refs = refs[: groups * groups], refs[groups * groups :]
    belief_ref, alphas_ref, values_ref, sems = refs
    group, _, _ = place()
    share = pieces[0].shape[0]
    for h in range(groups):

        @pl.when(group == h)
        def _(h=h):
            copies = []
            for d in range(groups):
                start = pl.multiple_of((group ^ d) * share, share)
                copies.append(
                    pltpu.make_async_copy(
                        pieces[h * groups + d], alphas_ref.at[pl.ds(start, share)], sems.at[d]
                    )
                )
            for copy in copies:
                copy.start()
            for copy in copies:
                copy.wait()

    product = belief_ref[...] * alphas_ref[...]
    values_ref[...] = lax.dot_general(
        jnp.ones((8, product.shape[1]), jnp.float32),
        product,
        (((1,), (1,)), ((), ())),
        precision=lax.Precision.HIGHEST,
        preferred_element_type=jnp.float32,
    )[0:1]


def local(belief, action, next_index, obs_table, transition, reward, terminal):
    groups = lax.axis_size("section")
    states = lax.axis_size("state")
    chips = states // 2
    group = lax.axis_index("section")
    beliefs, width = terminal.shape
    actions, observations = obs_table.shape[:2]
    share = beliefs // groups
    flat = transition.reshape(actions * width, transition.shape[2])

    own = jnp.concatenate(
        [jnp.transpose(next_index[0]), jnp.broadcast_to(action, (8, beliefs))], axis=0
    )
    index = []
    for d in range(groups):
        part = lax.dynamic_slice_in_dim(own, (group ^ d) * share, share, 1)
        index.append(part if d == 0 else swap(part, "section", d))

    def step(section, next_pieces):
        masked, send = pl.pallas_call(
            functools.partial(
                pick_kernel, section, groups, observations, actions, len(next_pieces) == 1
            ),
            out_shape=(
                jax.ShapeDtypeStruct((share, actions * width), jnp.bfloat16),
                jax.ShapeDtypeStruct((chips, share, width), jnp.float32),
            ),
            in_specs=[VMEM] * (groups + len(next_pieces) + 2),
            out_specs=(VMEM, VMEM),
            scratch_shapes=[
                pltpu.VMEM((128, 128), jnp.int32),
                pltpu.VMEM((beliefs, width), jnp.bfloat16),
            ],
            name="pick",
        )(*index, *next_pieces, obs_table, flat)
        other = swap(send, "state", 1)
        keep = pl.pallas_call(
            keep_kernel,
            out_shape=jax.ShapeDtypeStruct((chips, share, width), jnp.float32),
            in_specs=[VMEM, VMEM],
            out_specs=VMEM,
            name="keep",
        )(masked, flat)
        both = [keep[d] + other[d] for d in range(chips)]
        summed = both[0]
        arrived = {d: swap(both[d], "state", 2 * d) for d in reversed(range(1, chips))}
        for d in arrived:
            summed = summed + arrived[d]
        chosen = sum(
            jnp.where((group ^ section) == d, index[d][observations], 0) for d in range(groups)
        )
        rows = jnp.zeros((share, width), jnp.float32)
        for a in range(actions):
            rows = jnp.where((chosen == a)[:, None], reward[a][None, :], rows)
        alphas = rows + discount * summed
        return [alphas] + [swap(alphas, "section", d) for d in range(1, groups)]

    pieces = {}
    nextset = [terminal]
    for section in reversed(range(groups)):
        nextset = step(section, nextset)
        pieces[section] = nextset
    flat_pieces = [pieces[h][d] for h in range(groups) for d in range(groups)]
    alphas, values = pl.pallas_call(
        functools.partial(last_kernel, groups),
        out_shape=(
            jax.ShapeDtypeStruct((beliefs, width), jnp.float32),
            jax.ShapeDtypeStruct((1, beliefs), jnp.float32),
        ),
        in_specs=[ANY] * (groups * groups) + [VMEM],
        out_specs=(VMEM, VMEM),
        scratch_shapes=[pltpu.SemaphoreType.DMA((groups,))],
        name="last",
    )(*flat_pieces, belief[0])
    distance = 1
    while distance < states:
        values = values + swap(values, "state", distance)
        distance *= 2
    return alphas[None], values


def solution(mesh):
    return jax.shard_map(
        local,
        mesh=mesh,
        in_specs=(
            P("section", None, "state"),
            P("section", None),
            P("section", None, None),
            P(None, None, "state"),
            P(None, "state", None),
            P(None, "state"),
            P(None, "state"),
        ),
        out_specs=(P("section", None, "state"), P("section", None)),
        check_vma=False,
    )
```

```python
import functools

import jax
import jax.numpy as jnp
from jax import lax
from jax.experimental import pallas as pl
from jax.experimental.pallas import tpu as pltpu
from jax.sharding import PartitionSpec as P

discount = 0.95


VMEM = pl.BlockSpec(memory_space=pltpu.VMEM)
SMALL = pltpu.CompilerParams(vmem_limit_bytes=24 << 20)
ANY = pl.BlockSpec(memory_space=pl.ANY)


def near(x):
    return pltpu.with_memory_space_constraint(x, pltpu.VMEM)


def swap(x, axis, distance):
    size = lax.axis_size(axis)
    return lax.ppermute(x, axis, [(i, i ^ distance) for i in range(size)])


def place():
    group = lax.axis_index("section")
    state = lax.axis_index("state")
    return group, state // 2, state % 2


def columns_of(t_ref, block, width):
    start = pl.multiple_of(block * width, width)
    return t_ref[:, pl.ds(start, width)]


def pick_kernel(section, groups, observations, actions, whole_next, *refs):
    index_refs, refs = refs[:groups], refs[groups:]
    next_count = 1 if whole_next else groups
    next_refs, refs = refs[:next_count], refs[next_count:]
    obs_ref, t_ref, masked_ref, send_ref, chosen_ref, index_scratch, next_scratch = refs
    group, chip, core = place()
    share, width = masked_ref.shape[0], obs_ref.shape[2]
    for d in range(groups):

        @pl.when((group ^ section) == d)
        def _(d=d):
            index_scratch[0 : observations + 8, 0:share] = index_refs[d][...]

    if whole_next:
        next_scratch[...] = next_refs[0][...].astype(jnp.bfloat16)
    else:
        for d in range(groups):
            start = pl.multiple_of((group ^ d) * share, share)
            next_scratch[pl.ds(start, share), :] = next_refs[d][...].astype(jnp.bfloat16)
    rows = jnp.transpose(index_scratch[...])[0:share]
    chosen = rows[:, observations : observations + 1]
    chosen_ref[...] = chosen
    names = lax.broadcasted_iota(jnp.int32, (share, next_scratch.shape[0]), 1)
    kinds = lax.broadcasted_iota(jnp.int32, (share, 2 * actions), 1)
    action_hot = ((kinds == chosen) | (kinds == chosen + actions)).astype(jnp.bfloat16)
    next_rows = next_scratch[...]
    total = jnp.zeros((share, width), jnp.float32)
    for o in range(observations):
        hot = (names == rows[:, o : o + 1]).astype(jnp.float32).astype(jnp.bfloat16)
        picked = jnp.dot(hot, next_rows, preferred_element_type=jnp.float32)
        table = obs_ref[:, o, :]
        high = table.astype(jnp.bfloat16)
        low = (table - high.astype(jnp.float32)).astype(jnp.bfloat16)
        weights = jnp.dot(
            action_hot, jnp.concatenate([high, low], axis=0), preferred_element_type=jnp.float32
        )
        total = total + picked * weights
    for a in range(actions):
        masked_ref[:, a * width : (a + 1) * width] = jnp.where(chosen == a, total, 0.0).astype(
            jnp.bfloat16
        )
    masked = masked_ref[...]
    for d in range(send_ref.shape[0]):
        send_ref[d] = jnp.dot(
            masked,
            columns_of(t_ref, (chip ^ d) * 2 + (1 - core), width),
            preferred_element_type=jnp.float32,
        )


def keep_kernel(actions, masked_ref, t_ref, chosen_ref, reward_ref, keep_ref, rows_ref):
    _, chip, core = place()
    rows = jnp.zeros(rows_ref.shape, jnp.float32)
    for a in range(actions):
        rows = jnp.where(chosen_ref[...] == a, reward_ref[a : a + 1, :], rows)
    rows_ref[...] = rows
    masked = masked_ref[...]
    for d in range(keep_ref.shape[0]):
        keep_ref[d] = jnp.dot(
            masked,
            columns_of(t_ref, (chip ^ d) * 2 + core, keep_ref.shape[2]),
            preferred_element_type=jnp.float32,
        )


def last_kernel(groups, *refs):
    pieces, refs = refs[: groups * groups], refs[groups * groups :]
    belief_ref, alphas_ref, values_ref, sems = refs
    group, _, _ = place()
    share = pieces[0].shape[0]
    for h in range(groups):

        @pl.when(group == h)
        def _(h=h):
            copies = []
            for d in range(groups):
                start = pl.multiple_of((group ^ d) * share, share)
                copies.append(
                    pltpu.make_async_copy(
                        pieces[h * groups + d], alphas_ref.at[pl.ds(start, share)], sems.at[d]
                    )
                )
            for copy in copies:
                copy.start()
            for copy in copies:
                copy.wait()

    product = belief_ref[...] * alphas_ref[...]
    values_ref[...] = lax.dot_general(
        jnp.ones((8, product.shape[1]), jnp.float32),
        product,
        (((1,), (1,)), ((), ())),
        precision=lax.Precision.HIGHEST,
        preferred_element_type=jnp.float32,
    )[0:1]


def local(belief, action, next_index, obs_table, transition, reward, terminal):
    groups = lax.axis_size("section")
    states = lax.axis_size("state")
    chips = states // 2
    group = lax.axis_index("section")
    beliefs, width = terminal.shape
    actions, observations = obs_table.shape[:2]
    share = beliefs // groups
    flat = transition.reshape(actions * width, transition.shape[2])

    own = jnp.concatenate(
        [jnp.transpose(next_index[0]), jnp.broadcast_to(action, (8, beliefs))], axis=0
    )
    index = []
    for d in range(groups):
        part = lax.dynamic_slice_in_dim(own, (group ^ d) * share, share, 1)
        index.append(part if d == 0 else swap(part, "section", d))

    def step(section, next_pieces):
        masked, send, chosen = pl.pallas_call(
            functools.partial(
                pick_kernel, section, groups, observations, actions, len(next_pieces) == 1
            ),
            out_shape=(
                pltpu.VMEM((share, actions * width), jnp.bfloat16),
                pltpu.VMEM((chips, share, width), jnp.float32),
                pltpu.VMEM((share, 1), jnp.int32),
            ),
            in_specs=[VMEM] * (groups + len(next_pieces) + 2),
            out_specs=(VMEM, VMEM, VMEM),
            scratch_shapes=[
                pltpu.VMEM((128, 128), jnp.int32),
                pltpu.VMEM((beliefs, width), jnp.bfloat16),
            ],
            compiler_params=SMALL,
            name="pick",
        )(*map(near, index), *map(near, next_pieces), near(obs_table), near(flat))
        other = swap(send, "state", 1)
        keep, rows = pl.pallas_call(
            functools.partial(keep_kernel, actions),
            out_shape=(
                pltpu.VMEM((chips, share, width), jnp.float32),
                pltpu.VMEM((share, width), jnp.float32),
            ),
            in_specs=[VMEM] * 4,
            out_specs=(VMEM, VMEM),
            compiler_params=SMALL,
            name="keep",
        )(near(masked), near(flat), near(chosen), near(reward))
        both = [keep[d] + other[d] for d in range(chips)]
        summed = both[0]
        arrived = {d: swap(both[d], "state", 2 * d) for d in reversed(range(1, chips))}
        for d in arrived:
            summed = summed + arrived[d]
        alphas = rows + discount * summed
        return [alphas] + [swap(alphas, "section", d) for d in range(1, groups)]

    pieces = {}
    nextset = [terminal]
    for section in reversed(range(groups)):
        nextset = step(section, nextset)
        pieces[section] = nextset
    flat_pieces = [pieces[h][d] for h in range(groups) for d in range(groups)]
    alphas, values = pl.pallas_call(
        functools.partial(last_kernel, groups),
        out_shape=(
            jax.ShapeDtypeStruct((beliefs, width), jnp.float32),
            jax.ShapeDtypeStruct((1, beliefs), jnp.float32),
        ),
        in_specs=[ANY] * (groups * groups) + [VMEM],
        out_specs=(VMEM, VMEM),
        scratch_shapes=[pltpu.SemaphoreType.DMA((groups,))],
        compiler_params=SMALL,
        name="last",
    )(*flat_pieces, near(belief[0]))
    distance = 1
    while distance < states:
        values = values + swap(values, "state", distance)
        distance *= 2
    return alphas[None], values


def solution(mesh):
    return jax.shard_map(
        local,
        mesh=mesh,
        in_specs=(
            P("section", None, "state"),
            P("section", None),
            P("section", None, None),
            P(None, None, "state"),
            P(None, "state", None),
            P(None, "state"),
            P(None, "state"),
        ),
        out_specs=(P("section", None, "state"), P("section", None)),
        check_vma=False,
    )
```

```python
import functools

import jax
import jax.numpy as jnp
from jax import lax
from jax.experimental import pallas as pl
from jax.experimental.pallas import tpu as pltpu
from jax.sharding import PartitionSpec as P

discount = 0.95
micro_batch = 128


VMEM = pl.BlockSpec(memory_space=pltpu.VMEM)
SMALL = pltpu.CompilerParams(vmem_limit_bytes=16 << 20)
HBM = pl.BlockSpec(memory_space=pltpu.HBM)


def near(x):
    return pltpu.with_memory_space_constraint(x, pltpu.VMEM)


def swap(x, axis, distance):
    size = lax.axis_size(axis)
    return lax.ppermute(x, axis, [(i, i ^ distance) for i in range(size)])


def place():
    group = lax.axis_index("section")
    state = lax.axis_index("state")
    return group, state // 2, state % 2


def times(masked, halves, block, width):
    start = pl.multiple_of(block * width, width)
    depth = halves[0].shape[0]
    total = None
    for k, half in enumerate(halves):
        part = jnp.dot(
            masked[:, k * depth : (k + 1) * depth],
            half[:, pl.ds(start, width)],
            preferred_element_type=jnp.float32,
        )
        total = part if total is None else total + part
    return total


def pack_kernel(groups, blocks, next_ref, action_ref, *piece_refs):
    group, _, _ = place()
    observations, beliefs = next_ref.shape
    length = beliefs // blocks
    rows = length // groups
    for d in range(groups):
        for k in range(groups):

            @pl.when((group ^ d) == k)
            def _(d=d, k=k):
                spans = [slice(m * length + k * rows, m * length + (k + 1) * rows) for m in range(blocks)]
                piece_refs[d][0:observations, :] = jnp.concatenate(
                    [next_ref[:, span] for span in spans], axis=1
                )
                piece_refs[d][observations:, :] = jnp.broadcast_to(
                    jnp.concatenate([action_ref[:, span] for span in spans], axis=1),
                    (8, rows * blocks),
                )


def stage_kernel(t_hbm, obs_hbm, terminal_hbm, t_ref, table_ref, next_ref, obs_ref, terminal_ref, sems):
    copies = [
        pltpu.make_async_copy(obs_hbm, obs_ref, sems.at[0]),
        pltpu.make_async_copy(terminal_hbm, terminal_ref, sems.at[1]),
        pltpu.make_async_copy(t_hbm.at[pl.ds(0, t_ref.shape[0])], t_ref, sems.at[2]),
    ]
    for copy in copies:
        copy.start()
    copies[0].wait()
    observations, width = obs_ref.shape[1:]
    for o in range(observations):
        row = obs_ref[:, o, :]
        high = row.astype(jnp.bfloat16)
        low = (row - high.astype(jnp.float32)).astype(jnp.bfloat16)
        table_ref[:, o * width : (o + 1) * width] = jnp.concatenate([high, low], axis=0)
    copies[1].wait()
    next_ref[...] = terminal_ref[...].astype(jnp.bfloat16)
    copies[2].wait()


def prep_kernel(section, groups, blocks, actions, first, *refs):
    index_refs, refs = refs[:groups], refs[groups:]
    table_ref, reward_ref, *refs = refs
    if first:
        t_hbm, *refs = refs
    hot_refs, refs = refs[:blocks], refs[blocks:]
    weights_ref, chosen_ref, rows_ref, *refs = refs
    if first:
        t_ref, index_scratch, sem = refs
        depth = t_ref.shape[0]
        copy = pltpu.make_async_copy(t_hbm.at[pl.ds(depth, depth)], t_ref, sem)
        copy.start()
    else:
        (index_scratch,) = refs
    group, _, _ = place()
    observations, share, width = weights_ref.shape
    count = share // blocks
    for d in range(groups):

        @pl.when((group ^ section) == d)
        def _(d=d):
            index_scratch[0 : observations + 8, 0:share] = index_refs[d][...]

    rows = jnp.transpose(index_scratch[...])[0:share]
    chosen = rows[:, observations : observations + 1]
    chosen_ref[...] = chosen
    reward_rows = jnp.zeros(rows_ref.shape, jnp.float32)
    for a in range(actions):
        reward_rows = jnp.where(chosen == a, reward_ref[a : a + 1, :], reward_rows)
    rows_ref[...] = reward_rows
    kinds = lax.broadcasted_iota(jnp.int32, (share, 2 * actions), 1)
    action_hot = ((kinds == chosen) | (kinds == chosen + actions)).astype(jnp.bfloat16)
    for o in range(observations):
        for m in range(blocks):
            named = hot_refs[m].shape[1]
            names = lax.broadcasted_iota(jnp.int32, (count, named), 1)
            hot_refs[m][o * count : (o + 1) * count, :] = (
                (names == rows[m * count : (m + 1) * count, o : o + 1])
                .astype(jnp.float32)
                .astype(jnp.bfloat16)
            )
        weights_ref[o] = jnp.dot(
            action_hot,
            table_ref[:, o * width : (o + 1) * width],
            preferred_element_type=jnp.float32,
        )
    if first:
        copy.wait()


def pick_kernel(groups, blocks, pieces, actions, *refs):
    piece_refs, refs = refs[:pieces], refs[pieces:]
    hot_refs, refs = refs[:blocks], refs[blocks:]
    weights_ref, chosen_ref, low_ref, high_ref, masked_ref, send_ref, next_scratch = refs
    group, chip, core = place()
    observations, share, width = weights_ref.shape
    count = share // blocks
    length = count * groups
    if pieces == 1:
        next_rows = piece_refs[0]
    else:
        next_rows = next_scratch
        for d in range(groups):
            for m in range(blocks):
                start = pl.multiple_of(m * length + (group ^ d) * count, count)
                next_scratch[pl.ds(start, count), :] = piece_refs[d][
                    m * count : (m + 1) * count, :
                ].astype(jnp.bfloat16)
    chosen = chosen_ref[...]
    batch = max(1, 256 // count)
    while observations % batch:
        batch //= 2
    for m in range(blocks):
        named = hot_refs[m].shape[1]
        total = jnp.zeros((count, width), jnp.float32)
        mine = slice(m * count, (m + 1) * count)
        for first in range(0, observations, batch):
            picked = jnp.dot(
                hot_refs[m][first * count : (first + batch) * count, :],
                next_rows[0:named, :],
                preferred_element_type=jnp.float32,
            )
            for k in range(batch):
                total = total + picked[k * count : (k + 1) * count] * weights_ref[first + k, mine, :]
        for a in range(actions):
            masked_ref[mine, a * width : (a + 1) * width] = jnp.where(
                chosen[mine] == a, total, 0.0
            ).astype(jnp.bfloat16)
    masked = masked_ref[...]
    for d in range(send_ref.shape[0]):
        send_ref[d] = times(masked, (low_ref, high_ref), (chip ^ d) * 2 + (1 - core), width)


def keep_kernel(masked_ref, low_ref, high_ref, keep_ref):
    _, chip, core = place()
    masked = masked_ref[...]
    for d in range(keep_ref.shape[0]):
        keep_ref[d] = times(masked, (low_ref, high_ref), (chip ^ d) * 2 + core, keep_ref.shape[2])


def last_kernel(groups, blocks, *refs):
    pieces, refs = refs[: groups * groups], refs[groups * groups :]
    belief_ref, alphas_ref, values_ref = refs
    group, _, _ = place()
    count = pieces[0].shape[0] // blocks
    length = count * groups
    for h in range(groups):

        @pl.when(group == h)
        def _(h=h):
            for d in range(groups):
                for m in range(blocks):
                    start = m * length + (h ^ d) * count
                    alphas_ref[start : start + count, :] = pieces[h * groups + d][
                        m * count : (m + 1) * count, :
                    ]

    product = belief_ref[...] * alphas_ref[...]
    values_ref[...] = lax.dot_general(
        jnp.ones((8, product.shape[1]), jnp.float32),
        product,
        (((1,), (1,)), ((), ())),
        precision=lax.Precision.HIGHEST,
        preferred_element_type=jnp.float32,
    )[0:1]


def local(belief, action, next_index, obs_table, transition, reward, terminal):
    groups = lax.axis_size("section")
    states = lax.axis_size("state")
    chips = states // 2
    group = lax.axis_index("section")
    beliefs, width = terminal.shape
    actions, observations = obs_table.shape[:2]
    share = beliefs // groups
    blocks = beliefs // micro_batch
    if beliefs % micro_batch or micro_batch % (16 * groups):
        blocks = 1
    count = share // blocks
    flat = transition.reshape(actions * width, transition.shape[2])
    half = (flat.shape[0] // 2, flat.shape[1])
    far = pltpu.with_memory_space_constraint(flat, pltpu.HBM)

    packed = pl.pallas_call(
        functools.partial(pack_kernel, groups, blocks),
        out_shape=[pltpu.VMEM((observations + 8, share), jnp.int32)] * groups,
        in_specs=[VMEM] * 2,
        out_specs=[VMEM] * groups,
        compiler_params=SMALL,
        name="pack",
    )(jnp.transpose(next_index[0]), action)
    index = [packed[0]] + [swap(packed[d], "section", d) for d in range(1, groups)]

    low, table, first_near = pl.pallas_call(
        stage_kernel,
        out_shape=(
            pltpu.VMEM(half, flat.dtype),
            pltpu.VMEM((2 * actions, observations * width), jnp.bfloat16),
            pltpu.VMEM(terminal.shape, jnp.bfloat16),
        ),
        in_specs=[HBM] * 3,
        out_specs=(VMEM, VMEM, VMEM),
        scratch_shapes=[
            pltpu.VMEM(obs_table.shape, jnp.float32),
            pltpu.VMEM(terminal.shape, jnp.float32),
            pltpu.SemaphoreType.DMA((3,)),
        ],
        compiler_params=SMALL,
        name="stage",
    )(
        far,
        pltpu.with_memory_space_constraint(obs_table, pltpu.HBM),
        pltpu.with_memory_space_constraint(terminal, pltpu.HBM),
    )

    def prep(section, index):
        first = section == groups - 1
        outs = [
            pltpu.VMEM((observations * count, (m + 1) * count * groups), jnp.bfloat16)
            for m in range(blocks)
        ]
        outs += [
            pltpu.VMEM((observations, share, width), jnp.float32),
            pltpu.VMEM((share, 1), jnp.int32),
            pltpu.VMEM((share, width), jnp.float32),
        ]
        scratch = [pltpu.VMEM((128, 128), jnp.int32)]
        if first:
            outs.append(pltpu.VMEM(half, flat.dtype))
            scratch.append(pltpu.SemaphoreType.DMA)
        return pl.pallas_call(
            functools.partial(prep_kernel, section, groups, blocks, actions, first),
            out_shape=outs,
            in_specs=[VMEM] * (groups + 2) + [HBM] * first,
            out_specs=[VMEM] * len(outs),
            scratch_shapes=scratch,
            compiler_params=SMALL,
            name="prep",
        )(*map(near, index), near(table), near(reward), *[far] * first)

    def step(section, next_pieces, ready):
        *hot, weights, chosen, rows = ready
        masked, send = pl.pallas_call(
            functools.partial(pick_kernel, groups, blocks, len(next_pieces), actions),
            out_shape=(
                pltpu.VMEM((share, actions * width), jnp.bfloat16),
                pltpu.VMEM((chips, share, width), jnp.float32),
            ),
            in_specs=[VMEM] * (len(next_pieces) + blocks + 4),
            out_specs=(VMEM, VMEM),
            scratch_shapes=[pltpu.VMEM((beliefs, width), jnp.bfloat16)],
            compiler_params=SMALL,
            name="pick",
        )(*map(near, (*next_pieces, *hot, weights, chosen, low, high)))
        other = swap(send, "state", 1)
        keep = pl.pallas_call(
            keep_kernel,
            out_shape=pltpu.VMEM((chips, share, width), jnp.float32),
            in_specs=[VMEM] * 3,
            out_specs=VMEM,
            compiler_params=SMALL,
            name="keep",
        )(near(masked), near(low), near(high))
        both = [keep[d] + other[d] for d in range(chips)]
        if section:
            *both, held = lax.optimization_barrier((*both, index[0]))
            ready = prep(section - 1, [held, *index[1:]])
        summed = both[0]
        arrived = [swap(both[d], "state", 2 * d) for d in reversed(range(1, chips))]
        for part in arrived:
            summed = summed + part
        alphas = rows + discount * summed
        return [alphas] + [swap(alphas, "section", d) for d in range(1, groups)], ready

    pieces = {}
    nextset = [first_near]
    *ready, high = prep(groups - 1, index)
    for section in reversed(range(groups)):
        nextset, ready = step(section, nextset, ready)
        pieces[section] = nextset
    flat_pieces = [pieces[h][d] for h in range(groups) for d in range(groups)]
    alphas, values = pl.pallas_call(
        functools.partial(last_kernel, groups, blocks),
        out_shape=(
            pltpu.VMEM((beliefs, width), jnp.float32),
            pltpu.VMEM((1, beliefs), jnp.float32),
        ),
        in_specs=[VMEM] * (groups * groups + 1),
        out_specs=(VMEM, VMEM),
        compiler_params=SMALL,
        name="last",
    )(*map(near, flat_pieces), near(belief[0]))
    distance = 1
    while distance < states:
        values = values + swap(values, "state", distance)
        distance *= 2
    return alphas[None], values


def solution(mesh):
    return jax.shard_map(
        local,
        mesh=mesh,
        in_specs=(
            P("section", None, "state"),
            P("section", None),
            P("section", None, None),
            P(None, None, "state"),
            P(None, "state", None),
            P(None, "state"),
            P(None, "state"),
        ),
        out_specs=(P("section", None, "state"), P("section", None)),
        check_vma=False,
    )
```
